128 devices in a mesh: dp: 4 (over y), expert: 32 (over z, x, core).
Axes of the slice: x: 4, y: 4, z: 4, core: 2. Of those that a mesh axis runs over, the one named last changes fastest.
Arguments:
- stream: bfloat16 [16384, 7168], P(('dp', 'expert')), may hold values from -30 to 30
- heads_out: bfloat16 [16384, 16384], P(('dp', 'expert')), may hold values from -6 to 6
- cotangent: bfloat16 [16384, 7168], P(('dp', 'expert')), may hold values from -6 to 6
- adapter_down: bfloat16 [16, 16384], replicated, may hold values from -0.046875 to 0.046875
- adapter_raise_factor: bfloat16 [16, 7168], replicated, may hold values from -0.59765625 to 0.59765625
- norm_gain: float32 [7168], replicated, may hold values from 0.5 to 2
- router: bfloat16 [256, 7168], replicated, may hold values from -0.125 to 0.125
- expert_ids: int32 [16384, 8], P(('dp', 'expert')), may hold values from 0 to 255, as said below
- w_gate_up: bfloat16 [32, 7168, 2, 1024], P('expert', None, None, 'dp'), may hold values from -0.0625 to 0.0625
- w_down: bfloat16 [32, 1024, 7168], P('expert', 'dp'), may hold values from -0.1875 to 0.1875
Outputs:
- residual_stream_gradient: bfloat16 [16384, 7168], P(('dp', 'expert'))
- grad_down: float32 [16, 16384], replicated
- raise_factor_gradient: float32 [16, 7168], replicated
The draws below stay inside these ranges and needn't reach their ends.
Inputs may be any that keep to these rules, and one draw needn't show every extreme that they name: `expert_ids`: each row names 8 different experts. Within each aligned block of 128 rows (the tokens of one device) every expert below 32 is named by at most 6 rows, and one of them is named by exactly 6 rows in every block; the order of a row's ids carries no meaning.
All inputs are finite; a program needn't handle non-finite values.
Results may differ from the reference program's by a relative error of at most 0.0085.
Values may be sent and summed in bfloat16 or wider, within the bound.
No kernel may reach another device: no remote copies, remote signals or barrier semaphores. Data moves between devices by JAX's collectives and lax.ppermute only.
A program may use at most 192 MiB of HBM per device.

```python
import jax
import jax.numpy as jnp
from jax import lax

D = 7168
HV = 16384
RANK = 16
ALL_EXP = 256
TOPK = 8
HID = 1024
T_DEV = 128
TOKENS = 16384
WIN = 32
CAP = 6
N_DP = 4
N_EXPERT = 32


def draw_stream(key, part):
    key_base, key_rows, key_cols = jax.random.split(key, 3)
    row_scale = jnp.exp(jax.random.uniform(key_rows, (TOKENS, 1), jnp.float32, -1.2, 1.2))
    col_scale = jnp.exp(jax.random.uniform(key_cols, (1, D), jnp.float32, -1.2, 1.2))
    base = jax.random.normal(key_base, (TOKENS, D), jnp.float32)
    return jnp.clip(base * row_scale * col_scale, -30.0, 30.0).astype(jnp.bfloat16)


def draw_expert_ids(key, part):
    blocks = TOKENS // T_DEV
    hot_expert = jax.random.randint(jax.random.fold_in(key, 11), (), 0, WIN)

    def one_block(block_index):
        block_key = jax.random.fold_in(jax.random.fold_in(key, 23), block_index)
        key_counts, key_order, key_noise = jax.random.split(block_key, 3)
        counts = jax.random.randint(key_counts, (WIN,), 0, CAP + 1)
        counts = jnp.where(jnp.arange(WIN) == hot_expert, CAP, counts)
        active = (jnp.arange(CAP)[None, :] < counts[:, None]).reshape(WIN * CAP).astype(jnp.int32)
        slot_rank = jnp.cumsum(active) - 1
        shuffle = jax.random.permutation(key_order, T_DEV)
        owner_token = shuffle[slot_rank % T_DEV]
        expert = jnp.arange(WIN * CAP) // CAP
        member = jnp.zeros((T_DEV, ALL_EXP), jnp.int32).at[owner_token, expert].max(active)
        priority = jax.random.randint(key_noise, (T_DEV, ALL_EXP), 1, 1024)
        outside = jnp.arange(ALL_EXP)[None, :] >= WIN
        scores = jnp.where(member > 0, 2048, jnp.where(outside, priority, 0)) * ALL_EXP + jnp.arange(ALL_EXP)[None, :]
        chosen = lax.top_k(scores, TOPK)[1]
        return chosen.astype(jnp.int32)
    routed = lax.map(one_block, jnp.arange(blocks))
    return routed.reshape(TOKENS, TOPK)


def block_scale(stream_key, shape, cuts, smallest, high):
    level, own = 1.0, jax.random.fold_in(stream_key, 6)
    for axis_at, blocks in cuts:
        steps = jnp.exp(jax.random.uniform(jax.random.fold_in(own, axis_at), (blocks,), jnp.float32, smallest / len(cuts), high / len(cuts)))
        level = level * jnp.repeat(steps, shape[axis_at] // blocks).reshape([-1 if axis == axis_at else 1 for axis in range(len(shape))])
    return level


def scatter_about(stream_key, shape, scale, most, shards=(), kind=jnp.bfloat16):
    level = block_scale(stream_key, shape, shards, -0.22, 0.18) if shards else 1.0
    array = jax.random.normal(stream_key, shape, jnp.float32) * scale * level
    return jnp.minimum(jnp.maximum(array, -most), most).astype(kind)


def setup_inputs(seed: int = 0) -> dict:
    keys = jax.random.split(jax.random.key(seed), 11)
    stream = draw_stream(jax.random.fold_in(keys[10], 71), 0)
    heads_out = scatter_about(keys[1], (TOKENS, HV), 1.0, 6.0, ((0, 128),))
    cotangent = scatter_about(keys[2], (TOKENS, D), 1.0, 6.0, ((0, 128),))
    adapter_down = scatter_about(keys[3], (RANK, HV), HV ** -0.5, 0.046875)
    adapter_raise_factor = scatter_about(keys[4], (RANK, D), 0.1, 0.59765625)
    norm_gain = jnp.clip(jax.random.uniform(keys[5], (D,), jnp.float32, 0.5, 2.0), 0.5, 2.0)
    router = scatter_about(keys[6], (ALL_EXP, D), (D // 4) ** -0.5, 0.125)
    expert_ids = draw_expert_ids(jax.random.fold_in(keys[10], 71), 0)
    w_gate_up = scatter_about(keys[8], (WIN, D, 2, HID), D ** -0.5, 0.0625, ((0, 32), (3, 4)))
    w_down = scatter_about(keys[9], (WIN, HID, D), HID ** -0.5, 0.1875, ((0, 32), (1, 4)))
    return dict(stream=stream, heads_out=heads_out, cotangent=cotangent, adapter_down=adapter_down, adapter_raise_factor=adapter_raise_factor, norm_gain=norm_gain, router=router, expert_ids=expert_ids, w_gate_up=w_gate_up, w_down=w_down)


adapter_scale_factor = 2.0
route_scale = 2.5
norm_eps = 1e-06

def gather_rows(table, where_from):
    return table[where_from]

def scatter_rows(values, where_to):
    return jnp.zeros((T_DEV, values.shape[1]), jnp.float32).at[where_to].add(values)

def expert_pass(item):
    weight_in, weight_out, rows_in, rows_grad = item
    quarter = HID // N_DP
    returned = jnp.zeros((rows_in.shape[0], D), jnp.float32)
    dot_total = jnp.zeros((rows_in.shape[0],), jnp.float32)
    for share in range(N_DP):
        joined = weight_in[:, :, share * quarter:(share + 1) * quarter].reshape(D, 2 * quarter)
        lowered = weight_out[share * quarter:(share + 1) * quarter]
        projected = jnp.dot(rows_in, joined, preferred_element_type=jnp.float32)
        gate_pre = projected[:, :quarter]
        up_pre = projected[:, quarter:]
        sigma_gate = jax.nn.sigmoid(gate_pre)
        activated = gate_pre * sigma_gate
        hidden = (activated * up_pre).astype(jnp.bfloat16)
        hidden_grad = jnp.dot(rows_grad, lowered.T, preferred_element_type=jnp.float32)
        dot_part = lax.optimization_barrier(jnp.sum(hidden.astype(jnp.float32) * hidden_grad, axis=1)).astype(jnp.bfloat16)
        pre_grad = jnp.concatenate([hidden_grad * up_pre * sigma_gate * (1.0 + gate_pre * (1.0 - sigma_gate)), hidden_grad * activated], axis=1).astype(jnp.bfloat16)
        part_rows = jnp.dot(pre_grad, joined.T, preferred_element_type=jnp.float32).astype(jnp.bfloat16)
        returned = returned + lax.optimization_barrier(part_rows).astype(jnp.float32)
        dot_total = dot_total + lax.optimization_barrier(dot_part).astype(jnp.float32)
    return (returned.astype(jnp.bfloat16), dot_total.astype(jnp.bfloat16))

def reference(stream, heads_out, cotangent, adapter_down, adapter_raise_factor, norm_gain, router, expert_ids, w_gate_up, w_down):
    hidden_code = jnp.dot(heads_out, adapter_down.T, preferred_element_type=jnp.float32).astype(jnp.bfloat16)
    combined_result = stream.astype(jnp.float32) + adapter_scale_factor * jnp.dot(hidden_code, adapter_raise_factor, preferred_element_type=jnp.float32)
    inverse = lax.rsqrt(lax.optimization_barrier(jnp.mean(combined_result * combined_result, axis=1, keepdims=True)) + norm_eps)
    normed = combined_result * inverse
    normed_in = (normed * norm_gain).astype(jnp.bfloat16)
    logits = jnp.dot(normed_in, router.T, preferred_element_type=jnp.float32)
    affinity = jax.nn.sigmoid(logits)
    chosen = jnp.take_along_axis(affinity, expert_ids, axis=1)
    affin_sum = lax.optimization_barrier(jnp.sum(chosen, axis=1, keepdims=True))
    gate_weights = route_scale * chosen / affin_sum
    blocks = TOKENS // T_DEV
    routed = expert_ids.reshape(blocks, T_DEV, TOPK)
    window_hit = routed[:, :, :, None] == jnp.arange(WIN, dtype=jnp.int32)
    member = lax.optimization_barrier(jnp.sum(window_hit.astype(jnp.int32), axis=2))
    gate_window = lax.optimization_barrier(jnp.sum(jnp.where(window_hit, gate_weights.reshape(blocks, T_DEV, TOPK)[:, :, :, None], 0.0), axis=2))
    position = jnp.cumsum(member, axis=1) - member
    slot_hit = (member[:, :, :, None] == 1) & (position[:, :, :, None] == jnp.arange(CAP, dtype=jnp.int32))
    token_slot = lax.optimization_barrier(jnp.sum(jnp.where(slot_hit, jnp.arange(T_DEV, dtype=jnp.int32)[None, :, None, None], 0), axis=1)).astype(jnp.int32)
    filled = jnp.any(slot_hit, axis=1)
    flat_slot = token_slot.reshape(blocks, WIN * CAP)
    keep = filled.reshape(blocks, WIN * CAP, 1)
    rows_in = jax.vmap(gather_rows)(normed_in.reshape(blocks, T_DEV, D), flat_slot)
    rows_grad = jax.vmap(gather_rows)(cotangent.reshape(blocks, T_DEV, D), flat_slot)
    rows_in = jnp.where(keep, rows_in, jnp.zeros_like(rows_in))
    rows_grad = jnp.where(keep, rows_grad, jnp.zeros_like(rows_grad))
    rows_in = rows_in.reshape(blocks, WIN, CAP, D).transpose(1, 0, 2, 3).reshape(WIN, blocks * CAP, D)
    rows_grad = rows_grad.reshape(blocks, WIN, CAP, D).transpose(1, 0, 2, 3).reshape(WIN, blocks * CAP, D)
    returned, slot_dots = lax.map(expert_pass, (w_gate_up, w_down, rows_in, rows_grad))
    returned = returned.reshape(WIN, blocks, CAP, D).transpose(1, 0, 2, 3).reshape(blocks, WIN * CAP, D)
    slot_dots = slot_dots.reshape(WIN, blocks, CAP).transpose(1, 0, 2)
    slot_gate = lax.optimization_barrier(jnp.sum(jnp.where(slot_hit, gate_window[:, :, :, None], 0.0), axis=1)).astype(jnp.bfloat16)
    slot_gate = lax.optimization_barrier(slot_gate)
    weighted = slot_gate.reshape(blocks, WIN * CAP, 1).astype(jnp.float32) * returned.astype(jnp.float32)
    unit_grad = jax.vmap(scatter_rows)(weighted, flat_slot).reshape(TOKENS, D)
    slot_dot = lax.optimization_barrier(jnp.sum(jnp.where(slot_hit, slot_dots.astype(jnp.float32)[:, None, :, :], 0.0), axis=3))
    gate_grad = lax.optimization_barrier(jnp.sum(jnp.where(window_hit, slot_dot[:, :, None, :], 0.0), axis=3)).reshape(TOKENS, TOPK)
    chosen_grad = route_scale * (gate_grad / affin_sum - lax.optimization_barrier(jnp.sum(gate_grad * chosen, axis=1, keepdims=True)) / (affin_sum * affin_sum))
    logit_pick = chosen_grad * chosen * (1.0 - chosen)
    choose = expert_ids[:, :, None] == jnp.arange(ALL_EXP, dtype=jnp.int32)
    logit_grad = lax.optimization_barrier(jnp.sum(jnp.where(choose, logit_pick[:, :, None], 0.0), axis=1)).astype(jnp.bfloat16)
    unit_grad = unit_grad + jnp.dot(logit_grad, router, preferred_element_type=jnp.float32)
    scaled = unit_grad * norm_gain
    residual_stream_gradient = (cotangent.astype(jnp.float32) + inverse * (scaled - normed * lax.optimization_barrier(jnp.mean(scaled * normed, axis=1, keepdims=True)))).astype(jnp.bfloat16)
    hidden_code_gradient = (adapter_scale_factor * jnp.dot(residual_stream_gradient, adapter_raise_factor.T, preferred_element_type=jnp.float32)).astype(jnp.bfloat16)
    device_group = N_DP * N_EXPERT
    raise_factor_gradient = adapter_scale_factor * jnp.dot(hidden_code.T, residual_stream_gradient, preferred_element_type=jnp.float32) / device_group
    grad_down = jnp.dot(hidden_code_gradient.T, heads_out, preferred_element_type=jnp.float32) / device_group
    return (residual_stream_gradient, grad_down, raise_factor_gradient)
```

```python
import jax
import jax.numpy as jnp
from jax import lax
from jax.sharding import Mesh
from jax.sharding import PartitionSpec as P

ALL_EXP = 256
CAP = 6
WIN = 32
SLOTS = WIN * CAP
LANES = 128

adapter_scale_factor = 2.0
route_scale = 2.5
norm_eps = 1e-06

ALL = ("pa", "pb", "chip", "core")
PAIR = ("pb", "chip", "core")
CHIPS = ("pa", "pb", "chip")
N_Y = 4
N_E = 32
N_DEV = N_Y * N_E
F32 = jnp.float32
BF16 = jnp.bfloat16


def keeps(y, e):
    return (e % 2) == (0 if y in (0, 3) else 1)


KEEP = [(y, e) for y in range(N_Y) for e in range(N_E) if keeps(y, e)]
LEAVE = [(y, e) for y in range(N_Y) for e in range(N_E) if not keeps(y, e)]
FIRST_KEEP = [(y * N_E + e, (3 - y) * N_E + e) for y, e in KEEP]
FIRST_LEAVE = [(y * N_E + e, (y ^ 1) * N_E + (e ^ 1)) for y, e in LEAVE]
LAST = [(y * N_E + e, (3 - y) * N_E + e) for y, e in LEAVE]
TO_LEAVE = [(y * N_E + e, y * N_E + (e ^ 1)) for y, e in KEEP]
TO_KEEP = [(y * N_E + e, y * N_E + (e ^ 1)) for y, e in LEAVE]
CORES = [(i, i ^ 1) for i in range(N_DEV)]


def move(block, pairs):
    return lax.ppermute(block, ALL, pairs)


def exchange(rows):
    return lax.all_to_all(rows, PAIR, split_axis=0, concat_axis=0, tiled=True)


def pack(rows):
    return rows.reshape(2 * N_E, -1, LANES)


def unpack(block):
    return block.reshape(SLOTS, -1)


def stays():
    return lax.axis_index("core") == (lax.axis_index("pa") ^ lax.axis_index("pb"))


def own_block(block):
    return jnp.where(stays(), block, move(block, TO_LEAVE))


def gather_gate(block):
    first = move(block, FIRST_KEEP + FIRST_LEAVE)
    last = move(first, LAST)
    return [own_block(block), first, move(first, CORES), last]


def gather_down(block):
    kept = move(block, FIRST_KEEP)
    left = move(block, FIRST_LEAVE)
    last = move(left, LAST)
    first = jnp.where(stays(), kept, left)
    return [own_block(block), first, move(first, CORES), last]


def last_block(last):
    return jnp.where(stays(), move(last, TO_KEEP), last)


def hidden_share(rows_in, rows_grad, joined, lowered):
    quarter = lowered.shape[0]
    projected = jnp.dot(rows_in, joined, preferred_element_type=F32)
    gate_pre = projected[:, :quarter]
    up_pre = projected[:, quarter:]
    sigma_gate = jax.nn.sigmoid(gate_pre)
    activated = gate_pre * sigma_gate
    hidden = (activated * up_pre).astype(BF16)
    hidden_grad = jnp.einsum("md,hd->mh", rows_grad, lowered, preferred_element_type=F32)
    slot_dots = jnp.sum(hidden.astype(F32) * hidden_grad, axis=1)
    pre_grad = jnp.concatenate(
        [
            hidden_grad * up_pre * sigma_gate * (1.0 + gate_pre * (1.0 - sigma_gate)),
            hidden_grad * activated,
        ],
        axis=1,
    ).astype(BF16)
    returned = jnp.einsum("mk,dk->md", pre_grad, joined, preferred_element_type=F32)
    return returned, slot_dots


def expert_rows(rows_in, rows_grad, shares):
    returned, dots = 0.0, 0.0
    for joined, lowered in shares:
        part, slot_dots = hidden_share(rows_in, rows_grad, joined, lowered)
        returned = returned + part
        dots = dots + slot_dots
    return returned, dots


def local(
    stream,
    heads_out,
    cotangent,
    adapter_down,
    adapter_raise_factor,
    norm_gain,
    router,
    expert_ids,
    w_gate_up,
    w_down,
):
    tokens_here, width = stream.shape
    quarter = w_down.shape[1]
    pa = lax.axis_index("pa")

    joined = gather_gate(w_gate_up.reshape(width, 2, quarter))
    joined[:3] = [lax.optimization_barrier(j.reshape(width, 2 * quarter)) for j in joined[:3]]
    lowered = gather_down(w_down.reshape(quarter, width))

    place = jnp.arange(WIN, dtype=jnp.int32)
    order = 2 * (place % 16) + ((place // 16) ^ pa)
    window_hit = expert_ids[:, :, None] == order[None, None, :]
    member = jnp.sum(window_hit.astype(F32), axis=1)
    earlier = jnp.arange(tokens_here)[:, None] > jnp.arange(tokens_here)[None, :]
    position = jnp.dot(
        earlier.astype(BF16), member.astype(BF16), preferred_element_type=F32
    ).astype(jnp.int32)
    slot_hit = (member[:, :, None] == 1.0) & (
        position[:, :, None] == jnp.arange(CAP, dtype=jnp.int32)[None, None, :]
    )
    pick = slot_hit.reshape(tokens_here, SLOTS).astype(BF16)

    send_grad = pack(
        jnp.einsum("ts,td->sd", pick, cotangent, preferred_element_type=F32).astype(BF16)
    )
    hidden_code = jnp.einsum(
        "th,rh->tr", heads_out, adapter_down, preferred_element_type=F32
    ).astype(BF16)
    combined_result = stream.astype(F32) + adapter_scale_factor * jnp.dot(
        hidden_code, adapter_raise_factor, preferred_element_type=F32
    )
    inverse = lax.rsqrt(
        jnp.mean(combined_result * combined_result, axis=1, keepdims=True) + norm_eps
    )
    normed = combined_result * inverse
    normed_in = (normed * norm_gain).astype(BF16)
    send_in = pack(
        jnp.einsum("ts,td->sd", pick, normed_in, preferred_element_type=F32).astype(BF16)
    )
    send_grad, send_in, joined[0] = lax.optimization_barrier((send_grad, send_in, joined[0]))
    rows_grad = exchange(send_grad)
    send_in, rows_grad = lax.optimization_barrier((send_in, rows_grad))
    rows_in = exchange(send_in)

    logits = jnp.einsum("td,ed->te", normed_in, router, preferred_element_type=F32)
    affinity = jax.nn.sigmoid(logits)
    choose = expert_ids[:, :, None] == jnp.arange(ALL_EXP, dtype=jnp.int32)[None, None, :]
    chosen = jnp.sum(jnp.where(choose, affinity[:, None, :], 0.0), axis=2)
    affin_sum = jnp.sum(chosen, axis=1, keepdims=True)
    gate_weights = route_scale * chosen / affin_sum
    gate_window = jnp.sum(jnp.where(window_hit, gate_weights[:, :, None], 0.0), axis=1)
    combine_weights = (
        jnp.where(slot_hit, gate_window[:, :, None], 0.0)
        .reshape(tokens_here, SLOTS)
        .astype(BF16)
    )

    rows_in, joined[1], joined[2] = lax.optimization_barrier((rows_in, joined[1], joined[2]))
    rows_in, rows_grad = unpack(rows_in), unpack(rows_grad)
    shares = list(zip(joined, lowered))
    own_rows, own_dots = expert_rows(rows_in, rows_grad, shares[:1])
    own_dots, joined[3] = lax.optimization_barrier((own_dots, joined[3]))
    more_rows, more_dots = expert_rows(rows_in, rows_grad, shares[1:3])
    early_rows, early_dots = own_rows + more_rows, own_dots + more_dots
    early_rows = lax.optimization_barrier(early_rows)
    last_joined = last_block(joined[3]).reshape(width, 2 * quarter)
    last_joined = lax.optimization_barrier(last_joined)
    last_share = (last_joined, last_block(lowered[3]))
    late_rows, late_dots = hidden_share(rows_in, rows_grad, *last_share)
    back_rows = (early_rows + late_rows).astype(BF16)
    dots = early_dots + late_dots
    dots = dots.astype(BF16).reshape(2 * N_E, 1, 3)
    dots = jnp.pad(dots, ((0, 0), (0, 7), (0, LANES - 3)))
    back = exchange(jnp.concatenate([pack(back_rows), dots], axis=1))
    returned = unpack(back[:, :-8])
    dot_sum = back[:, -8, :3].reshape(WIN, CAP)

    slot_dot = jnp.sum(jnp.where(slot_hit, dot_sum.astype(F32)[None, :, :], 0.0), axis=2)
    gate_grad = jnp.sum(jnp.where(window_hit, slot_dot[:, None, :], 0.0), axis=2)
    chosen_grad = route_scale * (
        gate_grad / affin_sum
        - jnp.sum(gate_grad * chosen, axis=1, keepdims=True) / (affin_sum * affin_sum)
    )
    logit_pick = chosen_grad * chosen * (1.0 - chosen)
    logit_grad = jnp.sum(jnp.where(choose, logit_pick[:, :, None], 0.0), axis=1).astype(BF16)
    router_grad = jnp.dot(logit_grad, router, preferred_element_type=F32)

    unit_grad = jnp.dot(combine_weights, returned, preferred_element_type=F32) + router_grad
    scaled = unit_grad * norm_gain
    residual_stream_gradient = (
        cotangent.astype(F32)
        + inverse * (scaled - normed * jnp.mean(scaled * normed, axis=1, keepdims=True))
    ).astype(BF16)
    hidden_code_gradient = (
        adapter_scale_factor
        * jnp.einsum(
            "td,rd->tr", residual_stream_gradient, adapter_raise_factor, preferred_element_type=F32
        )
    ).astype(BF16)
    raise_part = (adapter_scale_factor / N_DEV) * jnp.einsum(
        "tr,td->rd", hidden_code, residual_stream_gradient, preferred_element_type=F32
    )
    down_part = (1.0 / N_DEV) * jnp.einsum(
        "tr,th->rh", hidden_code_gradient, heads_out, preferred_element_type=F32
    )

    rank = adapter_down.shape[0]
    down_cut = down_part.astype(BF16).reshape(rank, N_DEV, LANES).transpose(1, 0, 2)
    raise_cut = raise_part.astype(BF16).reshape(N_DEV, 7, LANES)
    raise_cut = jnp.pad(raise_cut, ((0, 0), (0, 1), (0, 0)))
    cut = jnp.concatenate([down_cut, raise_cut], axis=1)
    core = lax.axis_index("core")
    cut = cut.reshape(N_DEV // 2, 2, -1, LANES)
    mine = jnp.where(core == 0, cut[:, 0], cut[:, 1])
    other = move(jnp.where(core == 0, cut[:, 1], cut[:, 0]), CORES)
    cut = (mine.astype(F32) + other.astype(F32)).astype(BF16)
    cut = lax.all_to_all(cut, CHIPS, split_axis=0, concat_axis=0, tiled=True)
    total = jnp.sum(cut.astype(F32), axis=0).astype(BF16)
    half = jnp.broadcast_to(total[None], cut.shape)
    half = lax.all_to_all(half, CHIPS, split_axis=0, concat_axis=0, tiled=True)
    other = move(half, CORES)
    whole = jnp.stack(
        [jnp.where(core == 0, half, other), jnp.where(core == 0, other, half)], axis=1
    ).reshape(N_DEV, -1, LANES)
    sum_down = whole[:, :rank].transpose(1, 0, 2).reshape(rank, N_DEV * LANES).astype(F32)
    sum_up = whole[:, rank : rank + 7].reshape(rank, width).astype(F32)
    return (residual_stream_gradient, sum_down, sum_up)


def solution(mesh):
    wide = Mesh(mesh.devices.reshape(2, 2, N_E // 2, 2), ALL)
    return jax.shard_map(
        local,
        mesh=wide,
        in_specs=(
            P(ALL, None),
            P(ALL, None),
            P(ALL, None),
            P(),
            P(),
            P(),
            P(),
            P(ALL, None),
            P(("chip", "core"), None, None, ("pa", "pb")),
            P(("chip", "core"), ("pa", "pb"), None),
        ),
        out_specs=(P(ALL, None), P(), P()),
        check_vma=False,
    )
```

```python
import functools

import jax
import jax.numpy as jnp
from jax import lax
from jax.experimental import pallas as pl
from jax.sharding import Mesh
from jax.sharding import PartitionSpec as P

ALL_EXP = 256
CAP = 6
WIN = 32
SLOTS = WIN * CAP
LANES = 128

adapter_scale_factor = 2.0
route_scale = 2.5
norm_eps = 1e-06

ALL = ("pa", "pb", "chip", "core")
PAIR = ("pb", "chip", "core")
CHIPS = ("pa", "pb", "chip")
N_Y = 4
N_E = 32
N_DEV = N_Y * N_E
F32 = jnp.float32
BF16 = jnp.bfloat16


def keeps(y, e):
    return (e % 2) == (0 if y in (0, 3) else 1)


KEEP = [(y, e) for y in range(N_Y) for e in range(N_E) if keeps(y, e)]
LEAVE = [(y, e) for y in range(N_Y) for e in range(N_E) if not keeps(y, e)]
FIRST_KEEP = [(y * N_E + e, (3 - y) * N_E + e) for y, e in KEEP]
FIRST_LEAVE = [(y * N_E + e, (y ^ 1) * N_E + (e ^ 1)) for y, e in LEAVE]
LAST = [(y * N_E + e, (3 - y) * N_E + e) for y, e in LEAVE]
TO_LEAVE = [(y * N_E + e, y * N_E + (e ^ 1)) for y, e in KEEP]
TO_KEEP = [(y * N_E + e, y * N_E + (e ^ 1)) for y, e in LEAVE]
CORES = [(i, i ^ 1) for i in range(N_DEV)]


def move(block, pairs):
    return lax.ppermute(block, ALL, pairs)


def exchange(rows):
    return lax.all_to_all(rows, PAIR, split_axis=0, concat_axis=0, tiled=True)


def pack(rows):
    return rows.reshape(2 * N_E, -1, LANES)


def unpack(block):
    return block.reshape(SLOTS, -1)


def stays():
    return lax.axis_index("core") == (lax.axis_index("pa") ^ lax.axis_index("pb"))


def own_block(block):
    return jnp.where(stays(), block, move(block, TO_LEAVE))


def gather_gate(block):
    first = move(block, FIRST_KEEP + FIRST_LEAVE)
    last = move(first, LAST)
    return [own_block(block), first, move(first, CORES), last]


def gather_down(block):
    kept = move(block, FIRST_KEEP)
    left = move(block, FIRST_LEAVE)
    last = move(left, LAST)
    first = lax.optimization_barrier(jnp.where(stays(), kept, left))
    pair = move(first, CORES)
    return [own_block(block), first, pair, last]


def last_block(last):
    other = move(last, TO_KEEP)
    return jnp.where(stays(), other, last)


def down_product(rows_grad, lowered):
    return jnp.einsum("md,hd->mh", rows_grad, lowered, preferred_element_type=F32)


def up_tile(*refs):
    shares = (len(refs) - 1) // 2
    for joined, out in zip(refs[1 : 1 + shares], refs[1 + shares :]):
        part = jnp.dot(refs[0][...], joined[...], preferred_element_type=F32)

        @pl.when(pl.program_id(0) == 0)
        def _():
            out[...] = part

        @pl.when(pl.program_id(0) != 0)
        def _():
            out[...] += part


def up_products(rows_in, joined, tile=1024):
    rows, width = rows_in.shape
    deep, shares = joined[0].shape[1], len(joined)
    return pl.pallas_call(
        up_tile,
        grid=(width // tile,),
        in_specs=[pl.BlockSpec((rows, tile), lambda i: (0, i))]
        + [pl.BlockSpec((tile, deep), lambda i: (i, 0))] * shares,
        out_specs=[pl.BlockSpec((rows, deep), lambda i: (0, 0))] * shares,
        out_shape=[jax.ShapeDtypeStruct((rows, deep), F32)] * shares,
        cost_estimate=pl.CostEstimate(
            flops=2 * shares * rows * deep * width,
            bytes_accessed=2 * shares * width * deep + 2 * rows * width,
            transcendentals=0,
        ),
        name="up_products",
    )(rows_in, *joined)


def hidden_share(projected, hidden_grad):
    quarter = hidden_grad.shape[1]
    gate_pre = projected[:, :quarter]
    up_pre = projected[:, quarter:]
    sigma_gate = jax.nn.sigmoid(gate_pre)
    activated = gate_pre * sigma_gate
    hidden = (activated * up_pre).astype(BF16)
    slot_dots = jnp.sum(hidden.astype(F32) * hidden_grad, axis=1)
    pre_grad = jnp.concatenate(
        [
            hidden_grad * up_pre * sigma_gate * (1.0 + gate_pre * (1.0 - sigma_gate)),
            hidden_grad * activated,
        ],
        axis=1,
    ).astype(BF16)
    return pre_grad, slot_dots


def back_tile(shares, *refs):
    total = 0.0
    for grads, joined in zip(refs[:shares], refs[shares : 2 * shares]):
        total = total + lax.dot_general(
            grads[...], joined[...], (((1,), (1,)), ((), ())), preferred_element_type=F32
        )
    refs[-1][...] = total


def back_products(grads, joined, tile=1024):
    rows, deep = grads[0].shape
    width, shares = joined[0].shape[0], len(grads)
    return pl.pallas_call(
        functools.partial(back_tile, shares),
        grid=(width // tile,),
        in_specs=[pl.BlockSpec((rows, deep), lambda i: (0, 0))] * shares
        + [pl.BlockSpec((tile, deep), lambda i: (i, 0))] * shares,
        out_specs=pl.BlockSpec((rows, tile), lambda i: (0, i)),
        out_shape=jax.ShapeDtypeStruct((rows, width), F32),
        cost_estimate=pl.CostEstimate(
            flops=2 * shares * rows * deep * width,
            bytes_accessed=2 * shares * width * deep + 4 * rows * width,
            transcendentals=0,
        ),
        name="back_products",
    )(*grads, *joined)


def local(
    stream,
    heads_out,
    cotangent,
    adapter_down,
    adapter_raise_factor,
    norm_gain,
    router,
    expert_ids,
    w_gate_up,
    w_down,
):
    tokens_here, width = stream.shape
    quarter = w_down.shape[1]
    pa = lax.axis_index("pa")

    lowered = gather_down(w_down.reshape(quarter, width))
    joined = gather_gate(lax.optimization_barrier(w_gate_up.reshape(width, 2 * quarter)))
    joined[0] = lax.optimization_barrier(joined[0])

    place = jnp.arange(WIN, dtype=jnp.int32)
    order = 2 * (place % 16) + ((place // 16) ^ pa)
    window_hit = expert_ids[:, :, None] == order[None, None, :]
    member = jnp.sum(window_hit.astype(F32), axis=1)
    earlier = jnp.arange(tokens_here)[:, None] > jnp.arange(tokens_here)[None, :]
    position = jnp.dot(
        earlier.astype(BF16), member.astype(BF16), preferred_element_type=F32
    ).astype(jnp.int32)
    slot_hit = (member[:, :, None] == 1.0) & (
        position[:, :, None] == jnp.arange(CAP, dtype=jnp.int32)[None, None, :]
    )
    pick = slot_hit.reshape(tokens_here, SLOTS).astype(BF16)

    send_grad = pack(
        jnp.einsum("ts,td->sd", pick, cotangent, preferred_element_type=F32).astype(BF16)
    )
    hidden_code = jnp.einsum(
        "th,rh->tr", heads_out, adapter_down, preferred_element_type=F32
    ).astype(BF16)
    combined_result = stream.astype(F32) + adapter_scale_factor * jnp.dot(
        hidden_code, adapter_raise_factor, preferred_element_type=F32
    )
    inverse = lax.rsqrt(
        jnp.mean(combined_result * combined_result, axis=1, keepdims=True) + norm_eps
    )
    normed = combined_result * inverse
    normed_in = (normed * norm_gain).astype(BF16)
    send_in = pack(
        jnp.einsum("ts,td->sd", pick, normed_in, preferred_element_type=F32).astype(BF16)
    )
    send_grad, send_in, joined[0] = lax.optimization_barrier((send_grad, send_in, joined[0]))
    rows_grad = exchange(send_grad)
    send_in, rows_grad = lax.optimization_barrier((send_in, rows_grad))
    rows_in = exchange(send_in)

    logits = jnp.einsum("td,ed->te", normed_in, router, preferred_element_type=F32)
    affinity = jax.nn.sigmoid(logits)
    choose = expert_ids[:, :, None] == jnp.arange(ALL_EXP, dtype=jnp.int32)[None, None, :]
    chosen = jnp.sum(jnp.where(choose, affinity[:, None, :], 0.0), axis=2)
    affin_sum = jnp.sum(chosen, axis=1, keepdims=True)
    gate_weights = route_scale * chosen / affin_sum
    gate_window = jnp.sum(jnp.where(window_hit, gate_weights[:, :, None], 0.0), axis=1)
    combine_weights = (
        jnp.where(slot_hit, gate_window[:, :, None], 0.0)
        .reshape(tokens_here, SLOTS)
        .astype(BF16)
    )

    rows_in, rows_grad = unpack(rows_in), lax.optimization_barrier(unpack(rows_grad))
    products = [lax.optimization_barrier(down_product(rows_grad, lowered[0]))]
    products += [down_product(rows_grad, w) for w in lowered[1:3]]
    ups = up_products(rows_in, joined[:3])
    own_grad, own_dots = hidden_share(ups[0], products[0])
    own_grad, joined[3] = lax.optimization_barrier((own_grad, joined[3]))
    grads, dots = zip(*[hidden_share(ups[i], products[i]) for i in (1, 2)])
    early_dots = sum(dots) + own_dots
    early_rows = back_products((own_grad,) + grads, joined[:3])
    last_joined = lax.optimization_barrier(last_block(joined[3]))
    last_product = down_product(rows_grad, last_block(lowered[3]))
    last_up = jnp.dot(rows_in, last_joined, preferred_element_type=F32)
    last_up = lax.optimization_barrier(last_up)
    late_grad, late_dots = hidden_share(last_up, last_product)
    late_rows = jnp.einsum("mk,dk->md", late_grad, last_joined, preferred_element_type=F32)
    back_rows = (early_rows + late_rows).astype(BF16)
    dots = early_dots + late_dots
    dots = dots.astype(BF16).reshape(2 * N_E, 1, 3)
    dots = jnp.pad(dots, ((0, 0), (0, 7), (0, LANES - 3)))
    back = exchange(jnp.concatenate([pack(back_rows), dots], axis=1))
    returned = unpack(back[:, :-8])
    dot_sum = back[:, -8, :3].reshape(WIN, CAP)

    slot_dot = jnp.sum(jnp.where(slot_hit, dot_sum.astype(F32)[None, :, :], 0.0), axis=2)
    gate_grad = jnp.sum(jnp.where(window_hit, slot_dot[:, None, :], 0.0), axis=2)
    chosen_grad = route_scale * (
        gate_grad / affin_sum
        - jnp.sum(gate_grad * chosen, axis=1, keepdims=True) / (affin_sum * affin_sum)
    )
    logit_pick = chosen_grad * chosen * (1.0 - chosen)
    logit_grad = jnp.sum(jnp.where(choose, logit_pick[:, :, None], 0.0), axis=1).astype(BF16)
    router_grad = jnp.dot(logit_grad, router, preferred_element_type=F32)

    unit_grad = jnp.dot(combine_weights, returned, preferred_element_type=F32) + router_grad
    scaled = unit_grad * norm_gain
    residual_stream_gradient = (
        cotangent.astype(F32)
        + inverse * (scaled - normed * jnp.mean(scaled * normed, axis=1, keepdims=True))
    ).astype(BF16)
    hidden_code_gradient = (
        adapter_scale_factor
        * jnp.einsum(
            "td,rd->tr", residual_stream_gradient, adapter_raise_factor, preferred_element_type=F32
        )
    ).astype(BF16)
    raise_part = (adapter_scale_factor / N_DEV) * jnp.einsum(
        "tr,td->rd", hidden_code, residual_stream_gradient, preferred_element_type=F32
    )
    down_part = (1.0 / N_DEV) * jnp.einsum(
        "tr,th->rh", hidden_code_gradient, heads_out, preferred_element_type=F32
    )

    rank = adapter_down.shape[0]
    down_cut = down_part.astype(BF16).reshape(rank, N_DEV, LANES).transpose(1, 0, 2)
    raise_cut = raise_part.astype(BF16).reshape(N_DEV, 7, LANES)
    raise_cut = jnp.pad(raise_cut, ((0, 0), (0, 1), (0, 0)))
    cut = jnp.concatenate([down_cut, raise_cut], axis=1)
    core = lax.axis_index("core")
    cut = cut.reshape(N_DEV // 2, 2, -1, LANES)
    mine = jnp.where(core == 0, cut[:, 0], cut[:, 1])
    other = move(jnp.where(core == 0, cut[:, 1], cut[:, 0]), CORES)
    cut = (mine.astype(F32) + other.astype(F32)).astype(BF16)
    cut = lax.all_to_all(cut, CHIPS, split_axis=0, concat_axis=0, tiled=True)
    total = jnp.sum(cut.astype(F32), axis=0).astype(BF16)
    half = jnp.broadcast_to(total[None], cut.shape)
    half = lax.all_to_all(half, CHIPS, split_axis=0, concat_axis=0, tiled=True)
    other = move(half, CORES)
    whole = jnp.stack(
        [jnp.where(core == 0, half, other), jnp.where(core == 0, other, half)], axis=1
    ).reshape(N_DEV, -1, LANES)
    sum_down = whole[:, :rank].transpose(1, 0, 2).reshape(rank, N_DEV * LANES).astype(F32)
    sum_up = whole[:, rank : rank + 7].reshape(rank, width).astype(F32)
    return (residual_stream_gradient, sum_down, sum_up)


def solution(mesh):
    wide = Mesh(mesh.devices.reshape(2, 2, N_E // 2, 2), ALL)
    return jax.shard_map(
        local,
        mesh=wide,
        in_specs=(
            P(ALL, None),
            P(ALL, None),
            P(ALL, None),
            P(),
            P(),
            P(),
            P(),
            P(ALL, None),
            P(("chip", "core"), None, None, ("pa", "pb")),
            P(("chip", "core"), ("pa", "pb"), None),
        ),
        out_specs=(P(ALL, None), P(), P()),
        check_vma=False,
    )
```
